32 devices in a mesh: pb: 2 (over x), pair: 16 (over z, y, core).
Axes of the slice: x: 2, y: 2, z: 4, core: 2. Of those that a mesh axis runs over, the one named last changes fastest.
Arguments:
- screened: bfloat16 [32, 2048, 256], P(('pb', 'pair')), parts along dimension 0, may hold values from -0.1875 to 0.1875
- conduction: bfloat16 [20480, 2048], P(('pb', 'pair')), parts along dimension 0, may hold values from -6 to 6
- valence: bfloat16 [512, 2048], P(('pb', 'pair')), parts along dimension 0, may hold values from -0.125 to 0.125
- owners: int32 [8], P('pb'), parts along dimension 0, may hold values from 0 to 15, as said below
- column_block: int32 [8], P('pb'), parts along dimension 0, may hold values from 0 to 7
Outputs:
- kernel: bfloat16 [512, 10240], P('pb', 'pair'), parts along dimension 0
The draws below stay inside these ranges and needn't reach their ends.
There are 2 independent parts, one for each index of `pb`. The reference program is written for one: setup_inputs(seed, part) draws one part's arguments, and reference() takes and returns one part's arrays. A program takes and returns all parts, laid end to end along the dimension named above; each array names one. Nothing has to cross between parts.
Inputs may be any that keep to these rules, and one draw needn't show every extreme that they name: `owners`: the 4 entries are distinct devices of the group.
All inputs are finite; a program needn't handle non-finite values.
Results may differ from the reference program's by a relative error of at most 0.001.
Values may be sent and summed in bfloat16 or wider, within the bound.
A program may use at most 128 MiB of HBM per device.

```python
import jax
import jax.numpy as jnp
from jax import lax

NG = 2048
PW = 256
STEPS = 4
CPAIRS = 10240
VPAIRS = 256
N_PAIR = 16


def draw_owners(key, part):
    ordering = jax.random.permutation(jax.random.fold_in(key, 17), N_PAIR)
    return ordering[:STEPS].astype(jnp.int32)


def with_ends(values, own_key, least, top_value):
    dims = values.shape
    spot = [jax.random.randint(jax.random.fold_in(own_key, axis), (), 0, dims[axis]) for axis in range(len(dims))]
    values = values.at[tuple(spot)].set(least)
    longest = dims.index(max(dims))
    spot[longest] = (spot[longest] + 1) % dims[longest]
    return values.at[tuple(spot)].set(top_value)


def steps_of(key, extent, shards, low, high):
    def one(axis_at, shards_of):
        heights = jax.random.uniform(jax.random.fold_in(jax.random.fold_in(key, 6), axis_at), (shards_of,), jnp.float32, low / len(shards), high / len(shards))
        return jnp.repeat(jnp.exp(heights), extent[axis_at] // shards_of).reshape((-1,) + (1,) * (len(extent) - axis_at - 1))

    loudness = one(*shards[0])
    for cut in shards[1:]:
        loudness = loudness * one(*cut)
    return loudness


def centred(own_key, extent, deviation, most, pieces=(), held_as=jnp.bfloat16):
    level = steps_of(own_key, extent, pieces, -0.22, 0.18) if pieces else 1.0
    array = jax.random.normal(own_key, extent, jnp.float32) * deviation * level
    return jnp.minimum(jnp.maximum(array, -most), most).astype(held_as)


def setup_inputs(seed: int = 0, part: int = 0) -> dict:
    splits = jax.random.split(jax.random.key(seed), 6)
    part_keys = jax.random.split(jax.random.fold_in(splits[5], part), 6)
    screened = centred(part_keys[0], (N_PAIR, NG, PW), (STEPS * PW) ** -0.5, 0.1875, ((0, 16),))
    conduction = centred(part_keys[1], (CPAIRS, NG), 1.0, 6.0, ((0, 16),))
    valence = centred(part_keys[2], (VPAIRS, NG), NG ** -0.5, 0.125, ((0, 16),))
    owners = draw_owners(jax.random.fold_in(jax.random.fold_in(splits[5], part), 71), part)
    column_block = with_ends(jax.random.randint(part_keys[4], (STEPS,), 0, NG // PW), jax.random.fold_in(part_keys[4], 1), 0, (NG // PW) - 1).astype(jnp.int32)
    return dict(screened=screened, conduction=conduction, valence=valence, owners=owners, column_block=column_block)


def reference(screened, conduction, valence, owners, column_block):
    held_sum = jnp.zeros((conduction.shape[0], conduction.shape[1]), jnp.float32)
    for step_index in range(STEPS):
        panel_now = lax.dynamic_index_in_dim(screened, owners[step_index].astype(jnp.int32), 0, keepdims=False)
        first_col = (column_block[step_index] * PW).astype(jnp.int32)
        columns = lax.dynamic_slice_in_dim(conduction, first_col, PW, 1)
        held_sum = held_sum + jnp.dot(columns, panel_now.T, preferred_element_type=jnp.float32)
    result = jnp.dot(valence.astype(jnp.float32), held_sum.T, precision=lax.Precision.HIGHEST, preferred_element_type=jnp.float32)
    return result.astype(jnp.bfloat16)
```

```python
import functools

import jax
import jax.numpy as jnp
from jax import lax
from jax.experimental import pallas as pl
from jax.experimental.pallas import tpu as pltpu
from jax.sharding import PartitionSpec as P

MESH = pl.DeviceIdType.MESH
REACH = 3
PIECES = 1
LANES = 128
TOP = 32000.0
LOG2E = 1.4426950408889634
SPACE = pl.ANY


def grid_of(n):
    chips = n // 2
    b = 1
    while b * b * 4 <= chips:
        b *= 2
    return chips // b, b


def events_of(A, B):
    events = []
    for d in range(A):
        start = 1.0 * (-(-d // REACH)) + 0.3 * ((d - 1) % REACH if d else 0)
        last = start + 0.95 * (B - 1)
        for da in (1, -1) if d else (0,):
            for h in range(PIECES):
                when = start + 0.3 * h / PIECES
                events.append((when, 0, h, "a", d, da, 0, 0))
                for e in range(1, B):
                    for db in (1, -1):
                        events.append((when + 0.95 * e, 1, h, "b", d, da, e, db))
                for e in range(B):
                    for db in (1, -1) if e else (0,):
                        events.append((last + 0.75, 2, h, "core", d, da, e, db))
            events.append((last + 0.75, 3, 0, "group", d, da, 0, 0))
    return sorted(events, key=lambda ev: ev[:2])


def body(
    A, B, steps, pw,
    owners, blocks, valence, panel, conduction, out,
    v_all, pan, cond_v, cond_s, t_all, r_all, s_all,
    load_sems, p_send, p_recv, g1_recv, g1_a, g1_b, g1_c, g2_recv, g2_a, g2_b, g2_c, x_send, x_recv,
):
    n = A * B * 2
    chips = A * B
    rows, ng = valence.shape
    tiles = pw // LANES
    parcel = 2 * tiles + 1
    width = LANES // steps
    me = lax.axis_index("pair")
    c = lax.rem(me, 2)
    chip = lax.div(me, 2)
    b = lax.rem(chip, B)
    a = lax.div(chip, B)

    def at(aa, bb, cc):
        return (aa * B + bb) * 2 + cc

    def chip_of(idx):
        return lax.div(idx, 2)

    load_v = pltpu.make_async_copy(valence, v_all.at[chip], load_sems.at[0])
    load_p = pltpu.make_async_copy(panel.at[0], pan.at[c], load_sems.at[1])
    load_c = [
        pltpu.make_async_copy(conduction.at[:, pl.ds(k * pw, pw)], cond_v.at[k], load_sems.at[2 + k])
        for k in range(cond_v.shape[0])
    ]
    load_v.start()
    load_p.start()
    for load in load_c:
        load.start()

    barrier = pltpu.get_barrier_semaphore()
    near = [
        *((a >= hop, at(a - hop, b, c)) for hop in range(1, REACH + 1)),
        *((a + hop < A, at(a + hop, b, c)) for hop in range(1, REACH + 1)),
        (b > 0, at(a, b - 1, c)),
        (b < B - 1, at(a, b + 1, c)),
    ]
    count = jnp.int32(1)
    for there, who in near:
        count = count + there.astype(jnp.int32)

        @pl.when(there)
        def _():
            pl.semaphore_signal(barrier, inc=1, device_id={"pair": who}, device_id_type=MESH)

    twin = at(a, b, 1 - c)
    pl.semaphore_signal(barrier, inc=1, device_id={"pair": twin}, device_id_type=MESH)
    pl.semaphore_wait(barrier, count)

    def gather(view, recv, sem_a, sem_b, sem_c, on_group, cross, idle):
        def copy(idx, h, sem, who):
            return pltpu.make_async_remote_copy(
                src_ref=view(idx, h), dst_ref=view(idx, h), send_sem=sem, recv_sem=recv.at[h, idx],
                device_id={"pair": who}, device_id_type=MESH,
            )

        drains = []

        def send(cond, idx, h, sem, who):
            @pl.when(cond)
            def _():
                copy(idx, h, sem, who).start()

            def drain():
                @pl.when(cond)
                def _():
                    copy(idx, h, sem, who).wait_send()

            drains.append(drain)

        def arrived(idx, h):
            copy(idx, h, sem_a.at[h, 0, 0], me).wait_recv()

        first = True
        for _, _, h, kind, d, da, e, db in events_of(A, B):
            sa, sb = a - d * da, b - e * db
            there = (sa >= 0) & (sa < A) & (sb >= 0) & (sb < B)
            if kind == "a":
                idx = at(sa, b, c)
                if d:
                    @pl.when(there)
                    def _():
                        arrived(idx, h)
                for hop in range(1, REACH + 1) if d % REACH == 0 else ():
                    if da >= 0:
                        send(there & (a + hop < A), idx, h, sem_a.at[h, hop - 1, sa], at(a + hop, b, c))
                    if da <= 0:
                        send(there & (a >= hop), idx, h, sem_a.at[h, REACH - 1 + hop, sa], at(a - hop, b, c))
                send(there & (b < B - 1), idx, h, sem_b.at[h, 0, sa * B + b], at(a, b + 1, c))
                send(there & (b > 0), idx, h, sem_b.at[h, 1, sa * B + b], at(a, b - 1, c))
                if cross:
                    send(there, idx, h, sem_c.at[h, sa * B + b], twin)
            elif kind == "b":
                if first:
                    idle()
                    first = False
                idx = at(sa, sb, c)

                @pl.when(there)
                def _():
                    arrived(idx, h)

                if db > 0:
                    send(there & (b < B - 1), idx, h, sem_b.at[h, 0, sa * B + sb], at(a, b + 1, c))
                else:
                    send(there & (b > 0), idx, h, sem_b.at[h, 1, sa * B + sb], at(a, b - 1, c))
                if cross:
                    send(there, idx, h, sem_c.at[h, sa * B + sb], twin)
            elif kind == "core":
                if cross:
                    @pl.when(there)
                    def _():
                        arrived(at(sa, sb, 1 - c), h)
            else:
                @pl.when(there)
                def _():
                    on_group(sa)
        return drains

    group = 2 * B
    drains = []

    def exchange(dst):
        return pltpu.make_async_remote_copy(
            src_ref=t_all.at[pl.ds(dst * parcel, parcel)], dst_ref=r_all.at[pl.ds(chip * parcel, parcel)],
            send_sem=x_send.at[dst], recv_sem=x_recv.at[chip],
            device_id={"pair": dst * 2 + c}, device_id_type=MESH,
        )

    def contract_group(sa):
        first = sa * B
        height = B * rows
        left = v_all[pl.ds(first, B)].reshape(height, ng)
        lane = lax.broadcasted_iota(jnp.int32, (height, LANES), 1)
        levels = []
        for p in range(2):
            product = jnp.dot(left, pan[p], preferred_element_type=jnp.float32)
            top = jnp.maximum(jnp.max(jnp.abs(product), axis=1, keepdims=True), 1e-33)
            level = jnp.ceil(jnp.log(top) * LOG2E + 1e-3)
            scaled = product * (jnp.exp2(-level) * TOP)
            whole = (scaled + jnp.where(scaled >= 0, 0.5, -0.5)).astype(jnp.int32)
            for j in range(tiles):
                part = whole[:, j * LANES:(j + 1) * LANES].astype(jnp.int16)
                for k in range(B):
                    t_all[(first + k) * parcel + p * tiles + j] = part[k * rows:(k + 1) * rows]
            levels.append(jnp.broadcast_to(level.astype(jnp.int32), (height, LANES)))
        mark = jnp.where(lane < LANES // 2, levels[0], levels[1]).astype(jnp.int16)
        for k in range(B):
            t_all[(first + k) * parcel + 2 * tiles] = mark[k * rows:(k + 1) * rows]
        for k in range(B):
            dst = first + k

            @pl.when(dst != chip)
            def _():
                exchange(dst).start()

    def twin_panel():
        return pltpu.make_async_remote_copy(
            src_ref=pan.at[c], dst_ref=pan.at[c], send_sem=p_send.at[0], recv_sem=p_recv.at[0],
            device_id={"pair": twin}, device_id_type=MESH,
        )

    half_v = ng // PIECES

    def valence_view(idx, h):
        return v_all.at[chip_of(idx), :, pl.ds(h * half_v, half_v)]

    def chosen_view(idx, h):
        return s_all.at[idx]

    def settle():
        load_p.wait()
        twin_panel().start()
        for load in load_c:
            load.wait()
        for s in range(steps):
            cond_s[:, s * pw:(s + 1) * pw] = cond_v[blocks[s]]
        twin_panel().wait()

    load_v.wait()
    drains += gather(valence_view, g1_recv, g1_a, g1_b, g1_c, contract_group, False, settle)

    for k in range(parcel):
        r_all[chip * parcel + k] = t_all[chip * parcel + k]

    def take(k, carry):
        @pl.when(k != chip)
        def _():
            pltpu.make_async_remote_copy(
                src_ref=t_all.at[pl.ds(k * parcel, parcel)], dst_ref=r_all.at[pl.ds(k * parcel, parcel)],
                send_sem=x_send.at[k], recv_sem=x_recv.at[k],
                device_id={"pair": k * 2 + c}, device_id_type=MESH,
            ).wait_recv()
        return carry

    lax.fori_loop(0, chips, take, 0)
    lane = lax.broadcasted_iota(jnp.int32, (rows, LANES), 1)
    marks = jnp.zeros((rows, LANES), jnp.int32)
    for s in range(steps):
        who = owners[s]
        base = lax.div(who, 2) * parcel
        side = lax.rem(who, 2)
        for j in range(tiles):
            s_all[me, s * tiles + j] = r_all[base + side * tiles + j]
        both = r_all[base + 2 * tiles].astype(jnp.int32)
        odd = jnp.full((rows, LANES), side, jnp.int32) == 1
        level = jnp.where(
            odd,
            jnp.broadcast_to(both[:, LANES // 2:LANES // 2 + 1], (rows, LANES)),
            jnp.broadcast_to(both[:, 0:1], (rows, LANES)),
        )
        marks = jnp.where(lax.div(lane, width) == s, level, marks)
    s_all[me, steps * tiles] = marks.astype(jnp.int16)

    def output_group(sa):
        first = sa * group
        height = group * rows
        marks = s_all[pl.ds(first, group), steps * tiles].reshape(height, LANES)
        scale = jnp.exp2(marks.astype(jnp.int32).astype(jnp.float32)) * (1.0 / TOP)
        highs, lows = [], []
        for s in range(steps):
            factor = jnp.broadcast_to(scale[:, s * width:s * width + 1], (height, LANES))
            for j in range(tiles):
                value = s_all[pl.ds(first, group), s * tiles + j].reshape(height, LANES)
                value = value.astype(jnp.int32).astype(jnp.float32) * factor
                high = value.astype(jnp.bfloat16)
                highs.append(high)
                lows.append((value - high.astype(jnp.float32)).astype(jnp.bfloat16))
        left = jnp.concatenate([jnp.concatenate(highs, axis=1), jnp.concatenate(lows, axis=1)], axis=0)
        total = lax.dot_general(
            left, cond_s[...], (((1,), (1,)), ((), ())), preferred_element_type=jnp.float32
        )
        result = total[:height] + total[height:]
        out[pl.ds(pl.multiple_of(first * rows, height), height), :] = result.astype(out.dtype)

    drains += gather(chosen_view, g2_recv, g2_a, g2_b, g2_c, output_group, True, lambda: None)

    def drain_exchange(k, carry):
        @pl.when(k != chip)
        def _():
            exchange(k).wait_send()
        return carry

    lax.fori_loop(0, chips, drain_exchange, 0)
    for drain in drains:
        drain()


def solution(mesh):
    n = mesh.shape["pair"]
    A, B = grid_of(n)

    def per_device(screened, conduction, valence, owners, column_block):
        steps = owners.shape[0]
        rows, ng = valence.shape
        pw = screened.shape[2]
        cols = conduction.shape[0]
        chips = A * B
        parcel = 2 * (pw // LANES) + 1
        dma = pltpu.SemaphoreType.DMA
        sems = [dma((PIECES, n)), dma((PIECES, 2 * REACH, A)), dma((PIECES, 2, chips)), dma((PIECES, chips))]
        smem = pl.BlockSpec(memory_space=pltpu.SMEM)
        hbm = pl.BlockSpec(memory_space=SPACE)
        return pl.pallas_call(
            functools.partial(body, A, B, steps, pw),
            out_shape=jax.ShapeDtypeStruct((n * rows, cols), jnp.bfloat16),
            in_specs=[smem, smem, hbm, hbm, hbm],
            out_specs=pl.BlockSpec(memory_space=pltpu.VMEM),
            scratch_shapes=[
                pltpu.VMEM((chips, rows, ng), jnp.bfloat16),
                pltpu.VMEM((2, ng, pw), jnp.bfloat16),
                pltpu.VMEM((ng // pw, cols, pw), jnp.bfloat16),
                pltpu.VMEM((cols, steps * pw), jnp.bfloat16),
                pltpu.VMEM((chips * parcel, rows, LANES), jnp.int16),
                pltpu.VMEM((chips * parcel, rows, LANES), jnp.int16),
                pltpu.VMEM((n, steps * (pw // LANES) + 1, rows, LANES), jnp.int16),
                dma((2 + ng // pw,)),
                dma((1,)),
                dma((1,)),
                *sems,
                *sems,
                dma((chips,)),
                dma((chips,)),
            ],
            compiler_params=pltpu.CompilerParams(collective_id=0, has_side_effects=True),
            name="bse_direct",
        )(owners, column_block, valence, screened, conduction)

    placed = (
        P(("pb", "pair"), None, None),
        P(("pb", "pair"), None),
        P(("pb", "pair"), None),
        P("pb"),
        P("pb"),
    )
    return jax.shard_map(per_device, mesh=mesh, in_specs=placed, out_specs=P("pb", "pair"), check_vma=False)
```

```python
import functools

import jax
import jax.numpy as jnp
from jax import lax
from jax.experimental import pallas as pl
from jax.experimental.pallas import tpu as pltpu
from jax.sharding import PartitionSpec as P

MESH = pl.DeviceIdType.MESH
REACH = 3
PIECES = 1
LATE = 0.0
DIRECT = (1, 3)
LANES = 128
TOP = 32000.0
LOG2E = 1.4426950408889634
SPACE = pl.ANY


def grid_of(n):
    chips = n // 2
    b = 1
    while b * b * 4 <= chips:
        b *= 2
    return chips // b, b


def events_of(A, B, cross):
    events = []
    for d in range(A):
        start = 1.0 * (-(-d // REACH)) + 0.3 * ((d - 1) % REACH if d else 0)
        last = start + 0.95 * (B - 1)
        settled = last + (0.75 if cross else 0.0)
        for da in (1, -1) if d else (0,):
            for h in range(PIECES):
                when = start + 0.3 * h / PIECES
                events.append((when, 0, h, "a", d, da, 0, 0))
                for e in range(1, B):
                    for db in (1, -1):
                        events.append((when + 0.95 * e, 1, h, "b", d, da, e, db))
                if cross:
                    for e in range(B):
                        for db in (1, -1) if e else (0,):
                            events.append((settled, 2, h, "core", d, da, e, db))
            events.append((settled + LATE, 3, 0, "group", d, da, 0, 0))
    return sorted(events, key=lambda ev: ev[:2])


def body(
    A, B, steps, pw,
    owners, blocks, valence, panel, conduction, out,
    v_all, pan, cond_v, cond_s, t_all, r_all, s_all,
    load_sems, up, down, p_send, p_recv, g1_recv, g1_a, g1_b, g1_c, g1_d, g2_recv, g2_a, g2_b, g2_c, g2_d, x_send, x_recv,
):
    n = A * B * 2
    chips = A * B
    rows, ng = valence.shape
    tiles = pw // LANES
    parcel = 2 * tiles + 1
    width = LANES // steps
    me = lax.axis_index("pair")
    c = lax.rem(me, 2)
    chip = lax.div(me, 2)
    b = lax.rem(chip, B)
    a = lax.div(chip, B)

    def at(aa, bb, cc):
        return (aa * B + bb) * 2 + cc

    def chip_of(idx):
        return lax.div(idx, 2)

    load_v = pltpu.make_async_copy(valence, v_all.at[chip], load_sems.at[0])
    load_p = pltpu.make_async_copy(panel.at[0], pan.at[c], load_sems.at[1])
    load_c = [
        pltpu.make_async_copy(conduction.at[:, pl.ds(k * pw, pw)], cond_v.at[k], load_sems.at[2 + k])
        for k in range(cond_v.shape[0])
    ]
    load_v.start()
    load_p.start()
    for load in load_c:
        load.start()

    barrier = pltpu.get_barrier_semaphore()
    near = [
        (a > 0, at(a - 1, b, c)),
        (a < A - 1, at(a + 1, b, c)),
        (b > 0, at(a, b - 1, c)),
        (b < B - 1, at(a, b + 1, c)),
    ]
    count = jnp.int32(1)
    for there, who in near:
        count = count + there.astype(jnp.int32)

        @pl.when(there)
        def _():
            pl.semaphore_signal(barrier, inc=1, device_id={"pair": who}, device_id_type=MESH)

    twin = at(a, b, 1 - c)
    pl.semaphore_signal(barrier, inc=1, device_id={"pair": twin}, device_id_type=MESH)
    pl.semaphore_wait(barrier, count)

    def tell(hop):
        @pl.when((a > 0) & (a + hop - 1 < A))
        def _():
            pl.semaphore_signal(up.at[hop - 2], inc=1, device_id={"pair": at(a - 1, b, c)}, device_id_type=MESH)

        @pl.when((a < A - 1) & (a >= hop - 1))
        def _():
            pl.semaphore_signal(down.at[hop - 2], inc=1, device_id={"pair": at(a + 1, b, c)}, device_id_type=MESH)

    def hear(hop):
        @pl.when(a + hop < A)
        def _():
            pl.semaphore_wait(up.at[hop - 2], 1)

        @pl.when(a >= hop)
        def _():
            pl.semaphore_wait(down.at[hop - 2], 1)

    def gather(view, recv, sem_a, sem_b, sem_c, sem_d, on_group, cross, direct, staged):
        def copy(idx, h, sem, who):
            return pltpu.make_async_remote_copy(
                src_ref=view(idx, h), dst_ref=view(idx, h), send_sem=sem, recv_sem=recv.at[h, idx],
                device_id={"pair": who}, device_id_type=MESH,
            )

        drains = []

        def send(cond, idx, h, sem, who):
            @pl.when(cond)
            def _():
                copy(idx, h, sem, who).start()

            def drain():
                @pl.when(cond)
                def _():
                    copy(idx, h, sem, who).wait_send()

            drains.append(drain)

        def arrived(idx, h):
            copy(idx, h, sem_a.at[h, 0, 0], me).wait_recv()

        for _, _, h, kind, d, da, e, db in events_of(A, B, cross):
            sa, sb = a - d * da, b - e * db
            there = (sa >= 0) & (sa < A) & (sb >= 0) & (sb < B)
            if kind == "a":
                idx = at(sa, b, c)
                if d:
                    @pl.when(there)
                    def _():
                        arrived(idx, h)
                if d not in direct:
                    send(there & (b < B - 1), idx, h, sem_b.at[h, 0, sa * B + b], at(a, b + 1, c))
                    send(there & (b > 0), idx, h, sem_b.at[h, 1, sa * B + b], at(a, b - 1, c))
                first = staged is not None and d == 0 and h == 0
                order = range(1, REACH + 1)
                for hop in order if d % REACH == 0 else ():
                    if first and hop > 1:
                        staged(hop)
                    if da >= 0:
                        send(there & (a + hop < A), idx, h, sem_a.at[h, hop - 1, sa], at(a + hop, b, c))
                    if da <= 0:
                        send(there & (a >= hop), idx, h, sem_a.at[h, REACH - 1 + hop, sa], at(a - hop, b, c))
                    if d == 0 and hop in direct:
                        for way, db in enumerate((1, -1)):
                            beside = (b + db >= 0) & (b + db < B)
                            send(beside & (a + hop < A), idx, h, sem_d.at[h, way, hop - 1], at(a + hop, b + db, c))
                            send(beside & (a >= hop), idx, h, sem_d.at[h, way, REACH - 1 + hop], at(a - hop, b + db, c))
                if first:
                    staged(0)
                if cross:
                    send(there, idx, h, sem_c.at[h, sa * B + b], twin)
            elif kind == "b":
                idx = at(sa, sb, c)

                @pl.when(there)
                def _():
                    arrived(idx, h)

                if db > 0:
                    send(there & (b < B - 1), idx, h, sem_b.at[h, 0, sa * B + sb], at(a, b + 1, c))
                else:
                    send(there & (b > 0), idx, h, sem_b.at[h, 1, sa * B + sb], at(a, b - 1, c))
                if cross:
                    send(there, idx, h, sem_c.at[h, sa * B + sb], twin)
            elif kind == "core":
                if cross:
                    @pl.when(there)
                    def _():
                        arrived(at(sa, sb, 1 - c), h)
            else:
                if d == 0 and not cross:
                    twin_panel().wait_recv()

                @pl.when(there)
                def _():
                    on_group(sa)
        return drains

    group = 2 * B
    drains = []

    def exchange(dst):
        return pltpu.make_async_remote_copy(
            src_ref=t_all.at[pl.ds(dst * parcel, parcel)], dst_ref=r_all.at[pl.ds(chip * parcel, parcel)],
            send_sem=x_send.at[dst], recv_sem=x_recv.at[chip],
            device_id={"pair": dst * 2 + c}, device_id_type=MESH,
        )

    def contract_group(sa):
        first = sa * B
        height = B * rows
        left = v_all[pl.ds(first, B)].reshape(height, ng)
        lane = lax.broadcasted_iota(jnp.int32, (height, LANES), 1)
        levels = []
        for p in range(2):
            product = jnp.dot(left, pan[p], preferred_element_type=jnp.float32)
            top = jnp.maximum(jnp.max(jnp.abs(product), axis=1, keepdims=True), 1e-33)
            level = jnp.ceil(jnp.log(top) * LOG2E + 1e-3)
            scaled = product * (jnp.exp2(-level) * TOP)
            whole = (scaled + jnp.where(scaled >= 0, 0.5, -0.5)).astype(jnp.int32)
            for j in range(tiles):
                part = whole[:, j * LANES:(j + 1) * LANES].astype(jnp.int16)
                for k in range(B):
                    t_all[(first + k) * parcel + p * tiles + j] = part[k * rows:(k + 1) * rows]
            levels.append(jnp.broadcast_to(level.astype(jnp.int32), (height, LANES)))
        mark = jnp.where(lane < LANES // 2, levels[0], levels[1]).astype(jnp.int16)
        for k in range(B):
            t_all[(first + k) * parcel + 2 * tiles] = mark[k * rows:(k + 1) * rows]
        for k in range(B):
            dst = first + k

            @pl.when(dst != chip)
            def _():
                exchange(dst).start()

    def twin_panel():
        return pltpu.make_async_remote_copy(
            src_ref=pan.at[c], dst_ref=pan.at[c], send_sem=p_send.at[0], recv_sem=p_recv.at[0],
            device_id={"pair": twin}, device_id_type=MESH,
        )

    half_v = ng // PIECES

    def valence_view(idx, h):
        return v_all.at[chip_of(idx), :, pl.ds(h * half_v, half_v)]

    def chosen_view(idx, h):
        return s_all.at[idx]

    def staged(hop):
        if hop:
            hear(hop)
            if hop < REACH:
                tell(hop + 1)
        else:
            for load in load_c:
                load.wait()
            for s in range(steps):
                cond_s[:, s * pw:(s + 1) * pw] = cond_v[blocks[s]]

    tell(2)
    load_v.wait()
    load_p.wait()
    twin_panel().start()
    drains += gather(valence_view, g1_recv, g1_a, g1_b, g1_c, g1_d, contract_group, False, (), staged)

    for k in range(parcel):
        r_all[chip * parcel + k] = t_all[chip * parcel + k]

    def take(k, carry):
        @pl.when(k != chip)
        def _():
            pltpu.make_async_remote_copy(
                src_ref=t_all.at[pl.ds(k * parcel, parcel)], dst_ref=r_all.at[pl.ds(k * parcel, parcel)],
                send_sem=x_send.at[k], recv_sem=x_recv.at[k],
                device_id={"pair": k * 2 + c}, device_id_type=MESH,
            ).wait_recv()
        return carry

    lax.fori_loop(0, chips, take, 0)
    lane = lax.broadcasted_iota(jnp.int32, (rows, LANES), 1)
    marks = jnp.zeros((rows, LANES), jnp.int32)
    for s in range(steps):
        who = owners[s]
        base = lax.div(who, 2) * parcel
        side = lax.rem(who, 2)
        for j in range(tiles):
            s_all[me, s * tiles + j] = r_all[base + side * tiles + j]
        both = r_all[base + 2 * tiles].astype(jnp.int32)
        odd = jnp.full((rows, LANES), side, jnp.int32) == 1
        level = jnp.where(
            odd,
            jnp.broadcast_to(both[:, LANES // 2:LANES // 2 + 1], (rows, LANES)),
            jnp.broadcast_to(both[:, 0:1], (rows, LANES)),
        )
        marks = jnp.where(lax.div(lane, width) == s, level, marks)
    s_all[me, steps * tiles] = marks.astype(jnp.int16)

    def output_group(sa):
        first = sa * group
        height = group * rows
        marks = s_all[pl.ds(first, group), steps * tiles].reshape(height, LANES)
        scale = jnp.exp2(marks.astype(jnp.int32).astype(jnp.float32)) * (1.0 / TOP)
        highs, lows = [], []
        for s in range(steps):
            factor = jnp.broadcast_to(scale[:, s * width:s * width + 1], (height, LANES))
            for j in range(tiles):
                value = s_all[pl.ds(first, group), s * tiles + j].reshape(height, LANES)
                value = value.astype(jnp.int32).astype(jnp.float32) * factor
                high = value.astype(jnp.bfloat16)
                highs.append(high)
                lows.append((value - high.astype(jnp.float32)).astype(jnp.bfloat16))
        left = jnp.concatenate([jnp.concatenate(highs, axis=1), jnp.concatenate(lows, axis=1)], axis=0)
        total = lax.dot_general(
            left, cond_s[...], (((1,), (1,)), ((), ())), preferred_element_type=jnp.float32
        )
        result = total[:height] + total[height:]
        out[pl.ds(pl.multiple_of(first * rows, height), height), :] = result.astype(out.dtype)

    drains += gather(chosen_view, g2_recv, g2_a, g2_b, g2_c, g2_d, output_group, True, DIRECT, None)

    def drain_exchange(k, carry):
        @pl.when(k != chip)
        def _():
            exchange(k).wait_send()
        return carry

    twin_panel().wait_send()
    lax.fori_loop(0, chips, drain_exchange, 0)
    for drain in drains:
        drain()


def solution(mesh):
    n = mesh.shape["pair"]
    A, B = grid_of(n)

    def per_device(screened, conduction, valence, owners, column_block):
        steps = owners.shape[0]
        rows, ng = valence.shape
        pw = screened.shape[2]
        cols = conduction.shape[0]
        chips = A * B
        parcel = 2 * (pw // LANES) + 1
        dma = pltpu.SemaphoreType.DMA
        sems = [dma((PIECES, n)), dma((PIECES, 2 * REACH, A)), dma((PIECES, 2, chips)), dma((PIECES, chips)), dma((PIECES, 2, 2 * REACH))]
        smem = pl.BlockSpec(memory_space=pltpu.SMEM)
        hbm = pl.BlockSpec(memory_space=SPACE)
        return pl.pallas_call(
            functools.partial(body, A, B, steps, pw),
            out_shape=jax.ShapeDtypeStruct((n * rows, cols), jnp.bfloat16),
            in_specs=[smem, smem, hbm, hbm, hbm],
            out_specs=pl.BlockSpec(memory_space=pltpu.VMEM),
            scratch_shapes=[
                pltpu.VMEM((chips, rows, ng), jnp.bfloat16),
                pltpu.VMEM((2, ng, pw), jnp.bfloat16),
                pltpu.VMEM((ng // pw, cols, pw), jnp.bfloat16),
                pltpu.VMEM((cols, steps * pw), jnp.bfloat16),
                pltpu.VMEM((chips * parcel, rows, LANES), jnp.int16),
                pltpu.VMEM((chips * parcel, rows, LANES), jnp.int16),
                pltpu.VMEM((n, steps * (pw // LANES) + 1, rows, LANES), jnp.int16),
                dma((2 + ng // pw,)),
                pltpu.SemaphoreType.REGULAR((REACH - 1,)),
                pltpu.SemaphoreType.REGULAR((REACH - 1,)),
                dma((1,)),
                dma((1,)),
                *sems,
                *sems,
                dma((chips,)),
                dma((chips,)),
            ],
            compiler_params=pltpu.CompilerParams(collective_id=0, has_side_effects=True),
            name="bse_direct",
        )(owners, column_block, valence, screened, conduction)

    placed = (
        P(("pb", "pair"), None, None),
        P(("pb", "pair"), None),
        P(("pb", "pair"), None),
        P("pb"),
        P("pb"),
    )
    return jax.shard_map(per_device, mesh=mesh, in_specs=placed, out_specs=P("pb", "pair"), check_vma=False)
```

```python
import functools

import jax
import jax.numpy as jnp
from jax import lax
from jax.experimental import pallas as pl
from jax.experimental.pallas import tpu as pltpu
from jax.sharding import PartitionSpec as P

MESH = pl.DeviceIdType.MESH
REACH = 3
PIECES = 1
LATE = 0.1
DIRECT = (1, 3)
LANES = 128
TOP = 32000.0
LOG2E = 1.4426950408889634
SPACE = pl.ANY


def grid_of(n):
    chips = n // 2
    b = 1
    while b * b * 4 <= chips:
        b *= 2
    return chips // b, b


def events_of(A, B, cross, direct):
    events = []
    for d in range(A):
        start = 1.0 * (-(-d // REACH)) + 0.3 * ((d - 1) % REACH if d else 0)
        cast = 0.3 * REACH - 0.2 + 0.01 * d if d in direct else start
        last = cast + 0.95 * (B - 1)
        settled = last + (0.75 if cross else 0.0)
        for da in (1, -1) if d else (0,):
            for h in range(PIECES):
                when = start + 0.3 * h / PIECES
                events.append((when, 0, h, "a", d, da, 0, 0))
                for e in range(1, B):
                    for db in (1, -1):
                        events.append((cast + 0.3 * h / PIECES + 0.95 * e, 1, h, "b", d, da, e, db))
                if cross:
                    for e in range(B):
                        for db in (1, -1) if e else (0,):
                            events.append((settled, 2, h, "core", d, da, e, db))
            events.append((settled + (0.0 if d or cross else LATE), 3, 0, "group", d, da, 0, 0))
    return sorted(events, key=lambda ev: ev[:2])


def body(
    A, B, steps, pw,
    owners, blocks, valence, panel, conduction, out,
    v_all, pan, cond_v, cond_s, t_all, r_all, s_all,
    load_sems, up, down, p_send, p_recv, g1_recv, g1_a, g1_b, g1_c, g1_d, g2_recv, g2_a, g2_b, g2_c, g2_d, x_send, x_recv,
):
    n = A * B * 2
    chips = A * B
    rows, ng = valence.shape
    tiles = pw // LANES
    parcel = 2 * tiles + 1
    width = LANES // steps
    me = lax.axis_index("pair")
    c = lax.rem(me, 2)
    chip = lax.div(me, 2)
    b = lax.rem(chip, B)
    a = lax.div(chip, B)

    def at(aa, bb, cc):
        return (aa * B + bb) * 2 + cc

    def chip_of(idx):
        return lax.div(idx, 2)

    load_v = pltpu.make_async_copy(valence, v_all.at[chip], load_sems.at[0])
    load_p = pltpu.make_async_copy(panel.at[0], pan.at[c], load_sems.at[1])
    load_c = [
        pltpu.make_async_copy(conduction.at[:, pl.ds(k * pw, pw)], cond_v.at[k], load_sems.at[2 + k])
        for k in range(cond_v.shape[0])
    ]
    load_v.start()
    load_p.start()

    barrier = pltpu.get_barrier_semaphore()
    near = [
        (a > 0, at(a - 1, b, c)),
        (a < A - 1, at(a + 1, b, c)),
        (b > 0, at(a, b - 1, c)),
        (b < B - 1, at(a, b + 1, c)),
    ]
    count = jnp.int32(1)
    for there, who in near:
        count = count + there.astype(jnp.int32)

        @pl.when(there)
        def _():
            pl.semaphore_signal(barrier, inc=1, device_id={"pair": who}, device_id_type=MESH)

    twin = at(a, b, 1 - c)
    pl.semaphore_signal(barrier, inc=1, device_id={"pair": twin}, device_id_type=MESH)
    pl.semaphore_wait(barrier, count)
    for load in load_c:
        load.start()

    def tell(hop):
        @pl.when((a > 0) & (a + hop - 1 < A))
        def _():
            pl.semaphore_signal(up.at[hop - 2], inc=1, device_id={"pair": at(a - 1, b, c)}, device_id_type=MESH)

        @pl.when((a < A - 1) & (a >= hop - 1))
        def _():
            pl.semaphore_signal(down.at[hop - 2], inc=1, device_id={"pair": at(a + 1, b, c)}, device_id_type=MESH)

    def hear(hop):
        @pl.when(a + hop < A)
        def _():
            pl.semaphore_wait(up.at[hop - 2], 1)

        @pl.when(a >= hop)
        def _():
            pl.semaphore_wait(down.at[hop - 2], 1)

    def gather(view, recv, sem_a, sem_b, sem_c, sem_d, on_group, cross, direct, staged):
        def copy(idx, h, sem, who):
            return pltpu.make_async_remote_copy(
                src_ref=view(idx, h), dst_ref=view(idx, h), send_sem=sem, recv_sem=recv.at[h, idx],
                device_id={"pair": who}, device_id_type=MESH,
            )

        drains = []

        def send(cond, idx, h, sem, who):
            @pl.when(cond)
            def _():
                copy(idx, h, sem, who).start()

            def drain():
                @pl.when(cond)
                def _():
                    copy(idx, h, sem, who).wait_send()

            drains.append(drain)

        def arrived(idx, h):
            copy(idx, h, sem_a.at[h, 0, 0], me).wait_recv()

        for _, _, h, kind, d, da, e, db in events_of(A, B, cross, direct):
            sa, sb = a - d * da, b - e * db
            there = (sa >= 0) & (sa < A) & (sb >= 0) & (sb < B)
            if kind == "a":
                idx = at(sa, b, c)
                if d:
                    @pl.when(there)
                    def _():
                        arrived(idx, h)
                if d not in direct:
                    send(there & (b < B - 1), idx, h, sem_b.at[h, 0, sa * B + b], at(a, b + 1, c))
                    send(there & (b > 0), idx, h, sem_b.at[h, 1, sa * B + b], at(a, b - 1, c))
                first = staged is not None and d == 0 and h == 0
                order = range(1, REACH + 1)
                for hop in order if d % REACH == 0 else ():
                    if first and hop > 1:
                        staged(hop)
                    if da >= 0:
                        send(there & (a + hop < A), idx, h, sem_a.at[h, hop - 1, sa], at(a + hop, b, c))
                    if da <= 0:
                        send(there & (a >= hop), idx, h, sem_a.at[h, REACH - 1 + hop, sa], at(a - hop, b, c))
                    if d == 0 and hop in direct:
                        for way, db in enumerate((1, -1)):
                            beside = (b + db >= 0) & (b + db < B)
                            send(beside & (a + hop < A), idx, h, sem_d.at[h, way, hop - 1], at(a + hop, b + db, c))
                            send(beside & (a >= hop), idx, h, sem_d.at[h, way, REACH - 1 + hop], at(a - hop, b + db, c))
                if first:
                    staged(0)
                if cross:
                    send(there, idx, h, sem_c.at[h, sa * B + b], twin)
            elif kind == "b":
                idx = at(sa, sb, c)

                @pl.when(there)
                def _():
                    arrived(idx, h)

                if db > 0:
                    send(there & (b < B - 1), idx, h, sem_b.at[h, 0, sa * B + sb], at(a, b + 1, c))
                else:
                    send(there & (b > 0), idx, h, sem_b.at[h, 1, sa * B + sb], at(a, b - 1, c))
                if cross:
                    send(there, idx, h, sem_c.at[h, sa * B + sb], twin)
            elif kind == "core":
                if cross:
                    @pl.when(there)
                    def _():
                        arrived(at(sa, sb, 1 - c), h)
            else:
                if d == 0 and not cross:
                    twin_panel().wait_recv()

                @pl.when(there)
                def _():
                    on_group(sa)
        return drains

    group = 2 * B
    drains = []

    def exchange(dst):
        return pltpu.make_async_remote_copy(
            src_ref=t_all.at[pl.ds(dst * parcel, parcel)], dst_ref=r_all.at[pl.ds(chip * parcel, parcel)],
            send_sem=x_send.at[dst], recv_sem=x_recv.at[chip],
            device_id={"pair": dst * 2 + c}, device_id_type=MESH,
        )

    def contract_group(sa):
        first = sa * B
        height = B * rows
        left = v_all[pl.ds(first, B)].reshape(height, ng)
        lane = lax.broadcasted_iota(jnp.int32, (height, LANES), 1)
        levels = []
        for p in range(2):
            product = jnp.dot(left, pan[p], preferred_element_type=jnp.float32)
            top = jnp.maximum(jnp.max(jnp.abs(product), axis=1, keepdims=True), 1e-33)
            level = jnp.ceil(jnp.log(top) * LOG2E + 1e-3)
            scaled = product * (jnp.exp2(-level) * TOP)
            whole = (scaled + jnp.where(scaled >= 0, 0.5, -0.5)).astype(jnp.int32)
            for j in range(tiles):
                part = whole[:, j * LANES:(j + 1) * LANES].astype(jnp.int16)
                for k in range(B):
                    t_all[(first + k) * parcel + p * tiles + j] = part[k * rows:(k + 1) * rows]
            levels.append(jnp.broadcast_to(level.astype(jnp.int32), (height, LANES)))
        mark = jnp.where(lane < LANES // 2, levels[0], levels[1]).astype(jnp.int16)
        for k in range(B):
            t_all[(first + k) * parcel + 2 * tiles] = mark[k * rows:(k + 1) * rows]
        for k in range(B):
            dst = first + k

            @pl.when(dst != chip)
            def _():
                exchange(dst).start()

    def twin_panel():
        return pltpu.make_async_remote_copy(
            src_ref=pan.at[c], dst_ref=pan.at[c], send_sem=p_send.at[0], recv_sem=p_recv.at[0],
            device_id={"pair": twin}, device_id_type=MESH,
        )

    half_v = ng // PIECES

    def valence_view(idx, h):
        return v_all.at[chip_of(idx), :, pl.ds(h * half_v, half_v)]

    def chosen_view(idx, h):
        return s_all.at[idx]

    def staged(hop):
        if hop:
            if hop == 2:
                load_p.wait()
                twin_panel().start()
            hear(hop)
            if hop < REACH:
                tell(hop + 1)
        else:
            for load in load_c:
                load.wait()
            for s in range(steps):
                cond_s[s * pw:(s + 1) * pw, :] = cond_v[blocks[s]].T

    tell(2)
    load_v.wait()
    drains += gather(valence_view, g1_recv, g1_a, g1_b, g1_c, g1_d, contract_group, False, (), staged)

    for k in range(parcel):
        r_all[chip * parcel + k] = t_all[chip * parcel + k]

    def take(k, carry):
        @pl.when(k != chip)
        def _():
            pltpu.make_async_remote_copy(
                src_ref=t_all.at[pl.ds(k * parcel, parcel)], dst_ref=r_all.at[pl.ds(k * parcel, parcel)],
                send_sem=x_send.at[k], recv_sem=x_recv.at[k],
                device_id={"pair": k * 2 + c}, device_id_type=MESH,
            ).wait_recv()
        return carry

    lax.fori_loop(0, chips, take, 0)
    lane = lax.broadcasted_iota(jnp.int32, (rows, LANES), 1)
    marks = jnp.zeros((rows, LANES), jnp.int32)
    for s in range(steps):
        who = owners[s]
        base = lax.div(who, 2) * parcel
        side = lax.rem(who, 2)
        for j in range(tiles):
            s_all[me, s * tiles + j] = r_all[base + side * tiles + j]
        both = r_all[base + 2 * tiles].astype(jnp.int32)
        odd = jnp.full((rows, LANES), side, jnp.int32) == 1
        level = jnp.where(
            odd,
            jnp.broadcast_to(both[:, LANES // 2:LANES // 2 + 1], (rows, LANES)),
            jnp.broadcast_to(both[:, 0:1], (rows, LANES)),
        )
        marks = jnp.where(lax.div(lane, width) == s, level, marks)
    s_all[me, steps * tiles] = marks.astype(jnp.int16)

    def output_group(sa):
        first = sa * group
        height = group * rows
        marks = s_all[pl.ds(first, group), steps * tiles].reshape(height, LANES)
        scale = jnp.exp2(marks.astype(jnp.int32).astype(jnp.float32)) * (1.0 / TOP)
        highs, lows = [], []
        for s in range(steps):
            factor = jnp.broadcast_to(scale[:, s * width:s * width + 1], (height, LANES))
            for j in range(tiles):
                value = s_all[pl.ds(first, group), s * tiles + j].reshape(height, LANES)
                value = value.astype(jnp.int32).astype(jnp.float32) * factor
                high = value.astype(jnp.bfloat16)
                highs.append(high)
                lows.append((value - high.astype(jnp.float32)).astype(jnp.bfloat16))
        left = jnp.concatenate([jnp.concatenate(highs, axis=1), jnp.concatenate(lows, axis=1)], axis=0)
        total = lax.dot_general(
            left, cond_s[...], (((1,), (0,)), ((), ())), preferred_element_type=jnp.float32
        )
        result = total[:height] + total[height:]
        out[pl.ds(pl.multiple_of(first * rows, height), height), :] = result.astype(out.dtype)

    drains += gather(chosen_view, g2_recv, g2_a, g2_b, g2_c, g2_d, output_group, True, DIRECT, None)

    def drain_exchange(k, carry):
        @pl.when(k != chip)
        def _():
            exchange(k).wait_send()
        return carry

    twin_panel().wait_send()
    lax.fori_loop(0, chips, drain_exchange, 0)
    for drain in drains:
        drain()


def solution(mesh):
    n = mesh.shape["pair"]
    A, B = grid_of(n)

    def per_device(screened, conduction, valence, owners, column_block):
        steps = owners.shape[0]
        rows, ng = valence.shape
        pw = screened.shape[2]
        cols = conduction.shape[0]
        chips = A * B
        parcel = 2 * (pw // LANES) + 1
        dma = pltpu.SemaphoreType.DMA
        sems = [dma((PIECES, n)), dma((PIECES, 2 * REACH, A)), dma((PIECES, 2, chips)), dma((PIECES, chips)), dma((PIECES, 2, 2 * REACH))]
        smem = pl.BlockSpec(memory_space=pltpu.SMEM)
        hbm = pl.BlockSpec(memory_space=SPACE)
        return pl.pallas_call(
            functools.partial(body, A, B, steps, pw),
            out_shape=jax.ShapeDtypeStruct((n * rows, cols), jnp.bfloat16),
            in_specs=[smem, smem, hbm, hbm, hbm],
            out_specs=pl.BlockSpec(memory_space=pltpu.VMEM),
            scratch_shapes=[
                pltpu.VMEM((chips, rows, ng), jnp.bfloat16),
                pltpu.VMEM((2, ng, pw), jnp.bfloat16),
                pltpu.VMEM((ng // pw, cols, pw), jnp.bfloat16),
                pltpu.VMEM((steps * pw, cols), jnp.bfloat16),
                pltpu.VMEM((chips * parcel, rows, LANES), jnp.int16),
                pltpu.VMEM((chips * parcel, rows, LANES), jnp.int16),
                pltpu.VMEM((n, steps * (pw // LANES) + 1, rows, LANES), jnp.int16),
                dma((2 + ng // pw,)),
                pltpu.SemaphoreType.REGULAR((REACH - 1,)),
                pltpu.SemaphoreType.REGULAR((REACH - 1,)),
                dma((1,)),
                dma((1,)),
                *sems,
                *sems,
                dma((chips,)),
                dma((chips,)),
            ],
            compiler_params=pltpu.CompilerParams(collective_id=0, has_side_effects=True),
            name="bse_direct",
        )(owners, column_block, valence, screened, conduction)

    placed = (
        P(("pb", "pair"), None, None),
        P(("pb", "pair"), None),
        P(("pb", "pair"), None),
        P("pb"),
        P("pb"),
    )
    return jax.shard_map(per_device, mesh=mesh, in_specs=placed, out_specs=P("pb", "pair"), check_vma=False)
```
